32 devices in a mesh: dp: 16 (over z, y, core), tensor: 2 (over x).
Axes of the slice: x: 2, y: 2, z: 4, core: 2. Of those that a mesh axis runs over, the one named last changes fastest.
Arguments:
- tokens: bfloat16 [4096, 2048], P(('dp', 'tensor')), may hold values from -6 to 6
- segment_ids: int32 [16, 256], P('dp'), may hold values from 0 to 3, never falling along the last dimension, each value on 1 to 128 neighbouring positions
- ln1_gain: bfloat16 [2048], replicated, may hold values from 0.5 to 1.5
- ln1_bias: bfloat16 [2048], replicated, may hold values from -3 to 3
- w_qkv: bfloat16 [3, 2048, 2048], P(None, 'dp', 'tensor'), may hold values from -0.125 to 0.125
- b_qkv: bfloat16 [3, 2048], replicated, may hold values from -3 to 3
- w_out: bfloat16 [2048, 2048], P('tensor', 'dp'), may hold values from -0.5 to 0.5
- ln2_gain: bfloat16 [2048], replicated, may hold values from 0.5 to 1.5
- ln2_bias: bfloat16 [2048], replicated, may hold values from -3 to 3
- w_gate_up: bfloat16 [2, 2048, 5632], P(None, 'dp', 'tensor'), may hold values from -0.125 to 0.125
- w_down: bfloat16 [5632, 2048], P('tensor', 'dp'), may hold values from -0.078125 to 0.078125
- grad_out: bfloat16 [4096, 2048], P(('dp', 'tensor')), may hold values from -12 to 12
Outputs:
- output: bfloat16 [4096, 2048], P(('dp', 'tensor'))
- grad_tokens: bfloat16 [4096, 2048], P(('dp', 'tensor'))
- grad_ln1_gain: float32 [2048], replicated
- grad_ln1_bias: float32 [2048], replicated
- grad_w_qkv: float32 [3, 2048, 2048], P(None, 'dp', 'tensor')
- grad_b_qkv: float32 [3, 2048], replicated
- grad_w_out: float32 [2048, 2048], P('tensor', 'dp')
- grad_ln2_gain: float32 [2048], replicated
- grad_ln2_bias: float32 [2048], replicated
- grad_w_gate_up: float32 [2, 2048, 5632], P(None, 'dp', 'tensor')
- grad_w_down: float32 [5632, 2048], P('tensor', 'dp')
The draws below stay inside these ranges and needn't reach their ends.
Inputs may be any that keep to these rules, and one draw needn't show every extreme that they name: `segment_ids`: along each row the ids never fall; a document holds at most 128 tokens, and some document exactly that many.
All inputs are finite; a program needn't handle non-finite values.
Results may differ from the reference program's by a relative error of at most 0.014.
Values may be sent and summed in bfloat16 or wider, within the bound.
No kernel may reach another device: no remote copies, remote signals or barrier semaphores. Data moves between devices by JAX's collectives and lax.ppermute only.
A program may use at most 320 MiB of HBM per device.

```python
import math
import jax
import jax.numpy as jnp
import numpy as np
from jax import lax

D = 2048
HEADS = 32
HEAD_DIM = 64
FF = 5632
ROT_DIMS = 16
LEN = 256
TOKENS = 4096
N_DP = 16


def spiked(values, rng, source, target, parts, factor):
    def block_of(dim):
        return (jnp.arange(values.shape[dim]) // (values.shape[dim] // parts)).reshape((-1,) + (1,) * (values.ndim - 1 - dim))

    first = jax.random.permutation(rng, parts)[block_of(target)]
    far = (block_of(target) + parts // 2) % parts
    return jnp.where((block_of(source) == first) | (block_of(source) == far), factor * values, values)


def block_levels(own_key, dims, cuts, low, top_value):
    level, own = 1.0, jax.random.fold_in(own_key, 6)
    for dim, shards_of in cuts:
        steps = jnp.exp(jax.random.uniform(jax.random.fold_in(own, dim), (shards_of,), jnp.float32, low / len(cuts), top_value / len(cuts)))
        level = level * jnp.repeat(steps, dims[dim] // shards_of).reshape([-1 if axis == dim else 1 for axis in range(len(dims))])
    return level


def split_up(count, total, most, skew):
    loads = [(1 << 20) // math.isqrt(rank ** skew) + 1 for rank in range(2, count + 1)]
    surplus, counts = total - most - (count - 1), [1] * (count - 1)
    while surplus > 0:
        movable = [i for i in range(count - 1) if counts[i] < most]
        whole, left = sum([loads[i] for i in movable]), surplus
        for i in movable:
            addition = min(most - counts[i], max(1, left * loads[i] // whole), surplus)
            counts[i] = counts[i] + addition
            surplus = surplus - addition
    return np.array([most] + counts)


def uneven(stream_key, number_of, total, bound, slope):
    if number_of == 2:
        one = jax.random.randint(stream_key, (), max(1, total - bound), min(bound, total - 1) + 1)
        return jnp.stack([one, total - one])
    sizes = jnp.asarray(split_up(number_of, total, bound, slope), jnp.int32)
    pairs = (number_of - 1) // 2
    giver, receiver = sizes[1:1 + 2 * pairs:2], sizes[2:2 + 2 * pairs:2]
    slack = jnp.minimum(giver - 1, bound - receiver)
    moved = jax.random.randint(jax.random.fold_in(stream_key, 1), (pairs,), 0, 1 << 20) % (slack + 1)
    sizes = sizes.at[1:1 + 2 * pairs:2].set(giver - moved).at[2:2 + 2 * pairs:2].set(receiver + moved)
    return sizes[jax.random.permutation(jax.random.fold_in(stream_key, 2), number_of)]


def gaussian(key, shape, scale, limit, pieces=(), kind=jnp.bfloat16):
    drawn = jax.random.normal(key, shape, jnp.float32) * scale
    if len(pieces) > 0:
        drawn = block_levels(key, shape, pieces, -0.22, 0.18) * drawn
    return jnp.clip(drawn, min=-limit, max=limit).astype(kind)


def gaussian_with(rng, shape, deviation, limit, split, heavy, kind=jnp.bfloat16):
    entries = deviation * jax.random.normal(rng, shape, jnp.float32)
    if split:
        entries = entries * block_levels(rng, shape, split, -0.22, 0.18)
    return jnp.clip(spiked(entries, jax.random.fold_in(rng, 3), *heavy), -limit, limit).astype(kind)


def setup_inputs(seed: int = 0) -> dict:
    key_list = jax.random.split(jax.random.key(seed), 13)
    return {
        "tokens": gaussian(key_list[0], (TOKENS, D), 1.0, 6.0, ((0, 32),)),
        "segment_ids": jax.vmap(lambda own: jnp.searchsorted(jnp.cumsum(uneven(own, 4, LEN, LEN // 2, 0)), jnp.arange(LEN), side="right"))(jax.random.split(key_list[1], N_DP)).reshape((N_DP, LEN)).astype(jnp.int32),
        "ln1_gain": jnp.clip(1.0 + 0.1 * jax.random.normal(key_list[2], (D,), jnp.float32), 0.5, 1.5).astype(jnp.bfloat16),
        "ln1_bias": gaussian(key_list[3], (D,), 0.5, 3.0),
        "w_qkv": gaussian(key_list[4], (3, D, D), D ** -0.5, 0.125, ((1, 16), (2, 2))),
        "b_qkv": gaussian(key_list[5], (3, D), 0.5, 3.0),
        "w_out": gaussian(key_list[6], (D, D), (D // 16) ** -0.5, 0.5, ((0, 2), (1, 16))),
        "ln2_gain": jnp.clip(1.0 + 0.1 * jax.random.normal(key_list[7], (D,), jnp.float32), 0.5, 1.5).astype(jnp.bfloat16),
        "ln2_bias": gaussian(key_list[8], (D,), 0.5, 3.0),
        "w_gate_up": gaussian(key_list[9], (2, D, FF), D ** -0.5, 0.125, ((1, 16), (2, 2))),
        "w_down": gaussian(key_list[10], (FF, D), FF ** -0.5, 0.078125, ((0, 2), (1, 16))),
        "grad_out": gaussian_with(key_list[11], (TOKENS, D), 1.0, 12.0, ((0, 32),), (0, 1, 32, 2.75)),
    }


HIGHEST_PRECISION = lax.Precision.HIGHEST

@jax.custom_vjp
def low(v):
    return lax.optimization_barrier(v.astype(jnp.bfloat16)).astype(jnp.float32)

@jax.custom_vjp
def low_back(v):
    return v

def low_keep(v):
    return (low(v), None)

def low_pass(kept, grad):
    return (grad,)

def back_keep(v):
    return (v, None)

def back_low(kept, grad):
    return (low(grad),)
low.defvjp(low_keep, low_pass)
low_back.defvjp(back_keep, back_low)

def layer_norm(values, gain, shift):
    row_mean = lax.optimization_barrier(jnp.mean(values, axis=-1, keepdims=True))
    centred = values - row_mean
    variance = lax.optimization_barrier(jnp.mean(centred * centred, axis=-1, keepdims=True))
    return centred * lax.rsqrt(variance + 1e-05) * gain + shift

def segment_tables(segments):
    seq_length = segments.shape[0]
    earlier = lax.optimization_barrier(jnp.sum((segments[None, :] < segments[:, None]).astype(jnp.int32), axis=1))
    position = jnp.arange(seq_length, dtype=jnp.int32) - earlier
    halfway = ROT_DIMS // 2
    frequency = jnp.exp(jnp.arange(halfway, dtype=jnp.float32) * (-2.0 * math.log(10000.0) / ROT_DIMS))
    angles = position.astype(jnp.float32)[:, None] * frequency[None, :]
    token_order = jnp.arange(seq_length, dtype=jnp.int32)
    visible = (token_order[None, :] <= token_order[:, None]) & (segments[None, :] == segments[:, None])
    return (jnp.cos(angles)[:, None, :], jnp.sin(angles)[:, None, :], visible)

def rotate_heads(values, cosine, sine_table, direction):
    halfway = ROT_DIMS // 2
    first_part = values[..., :halfway]
    second_part = values[..., halfway:ROT_DIMS]
    rest_part = values[..., ROT_DIMS:]
    return jnp.concatenate([first_part * cosine - direction * second_part * sine_table, second_part * cosine + direction * first_part * sine_table, rest_part], axis=-1)

def attend(inputs):
    query_heads, key_heads, value_heads, segments = inputs
    cosine, sine_table, visible = segment_tables(segments)
    queries = low(rotate_heads(query_heads, cosine, sine_table, 1.0))
    key_rot = low(rotate_heads(key_heads, cosine, sine_table, 1.0))
    values = low(value_heads)
    scores = low_back(jnp.einsum('qhe,khe->hqk', queries, key_rot, precision=HIGHEST_PRECISION) * HEAD_DIM ** (-0.5))
    scores = jnp.where(visible[None], scores, -1e+30)
    attention = low(jax.nn.softmax(scores, axis=-1))
    context = jnp.einsum('hqk,khe->qhe', attention, values, precision=HIGHEST_PRECISION)
    return low_back(low(context))

def block_forward(weights, block_inputs):
    ln1_gain, ln1_bias, w_qkv, b_qkv, w_out, ln2_gain, ln2_bias, w_gate_up, w_down = weights
    inputs, segments = block_inputs
    group_count = inputs.shape[0]
    seq_length = inputs.shape[1]
    normed1 = low(layer_norm(inputs, ln1_gain, ln1_bias))
    projected = low_back(jnp.einsum('gtd,cde->gtce', normed1, w_qkv, precision=HIGHEST_PRECISION) + b_qkv)
    split_heads = projected.reshape(group_count, seq_length, 3, HEADS, HEAD_DIM)
    context = lax.map(jax.checkpoint(attend), (split_heads[:, :, 0], split_heads[:, :, 1], split_heads[:, :, 2], segments))
    attended = low_back(jnp.einsum('gtf,fd->gtd', context.reshape(group_count, seq_length, D), w_out, precision=HIGHEST_PRECISION))
    residual = inputs + attended
    normed2 = low(layer_norm(residual, ln2_gain, ln2_bias))
    gate_up = low_back(jnp.einsum('gtd,cdf->gtcf', normed2, w_gate_up, precision=HIGHEST_PRECISION))
    hidden = low(jax.nn.silu(gate_up[:, :, 0]) * gate_up[:, :, 1])
    return residual + jnp.einsum('gtf,fd->gtd', hidden, w_down, precision=HIGHEST_PRECISION)

def reference(tokens, segment_ids, ln1_gain, ln1_bias, w_qkv, b_qkv, w_out, ln2_gain, ln2_bias, w_gate_up, w_down, grad_out):
    group_size = math.gcd(N_DP, 4)
    group_total = N_DP // group_size
    weights = tuple((item.astype(jnp.float32) for item in (ln1_gain, ln1_bias, w_qkv, b_qkv, w_out, ln2_gain, ln2_bias, w_gate_up, w_down)))
    inputs = tokens.astype(jnp.float32).reshape(group_total, group_size, LEN, D)
    segments = segment_ids.reshape(group_total, group_size, LEN)

    def forward(block_tokens, block_weights):

        def one_group(block_inputs):
            return block_forward(block_weights, block_inputs)
        return lax.map(jax.checkpoint(one_group), (block_tokens, segments))
    outputs, pullback = jax.vjp(forward, inputs, weights)
    grad_inputs, grad_weights = pullback(grad_out.astype(jnp.float32).reshape(group_total, group_size, LEN, D))
    return (outputs.reshape(TOKENS, D).astype(jnp.bfloat16), grad_inputs.reshape(TOKENS, D).astype(jnp.bfloat16), grad_weights[0], grad_weights[1], grad_weights[2], grad_weights[3], grad_weights[4], grad_weights[5], grad_weights[6], grad_weights[7], grad_weights[8])
```

```python
import math

import jax
import jax.numpy as jnp
import numpy as np
from jax import lax
from jax.sharding import PartitionSpec as P

D = 2048
HEAD_DIM = 64
ROT_DIMS = 16
EPSILON = 1e-05
SWAP = [(0, 1), (1, 0)]
ROWS = (((0,), (0,)), ((), ()))
COLS = (((1,), (1,)), ((), ()))


def mm(a, b, dims=(((1,), (0,)), ((), ()))):
    return lax.dot_general(a, b, dims, preferred_element_type=jnp.float32)


def layer_forward(values, gain, shift):
    row_mean = jnp.mean(values, axis=-1, keepdims=True)
    centred = values - row_mean
    variance = jnp.mean(centred * centred, axis=-1, keepdims=True)
    inverse = lax.rsqrt(variance + EPSILON)
    normal = centred * inverse
    return (normal * gain.astype(jnp.float32) + shift.astype(jnp.float32), normal, inverse)


def layer_backward(grad_normed, normal, inverse, gain):
    scaled = grad_normed * gain.astype(jnp.float32)
    first_mean = jnp.mean(scaled, axis=-1, keepdims=True)
    second_mean = jnp.mean(scaled * normal, axis=-1, keepdims=True)
    return inverse * (scaled - first_mean - normal * second_mean)


def segment_tables(segments, order):
    earlier = jnp.sum((segments[None, :] < segments[:, None]).astype(jnp.int32), axis=1)
    position = order - earlier
    halfway = ROT_DIMS // 2
    frequency = jnp.exp(
        jnp.arange(halfway, dtype=jnp.float32) * (-2.0 * math.log(10000.0) / ROT_DIMS)
    )
    angles = position.astype(jnp.float32)[:, None] * frequency[None, :]
    visible = (order[None, :] <= order[:, None]) & (segments[None, :] == segments[:, None])
    return (jnp.cos(angles)[:, None, :], jnp.sin(angles)[:, None, :], visible)


def rotate_heads(values, cosine, sine_table, direction):
    halfway = ROT_DIMS // 2
    first_part = values[..., :halfway]
    second_part = values[..., halfway:ROT_DIMS]
    rest_part = values[..., ROT_DIMS:]
    return jnp.concatenate(
        [
            first_part * cosine - direction * second_part * sine_table,
            second_part * cosine + direction * first_part * sine_table,
            rest_part,
        ],
        axis=-1,
    )


def ring_order(chips):
    half = chips // 2
    return [0] + [2 * i + 1 for i in range(half)] + [2 * i for i in range(half - 1, 0, -1)]


def swap_tensor(v):
    return lax.ppermute(v, "tensor", SWAP)


def per_device(
    tokens,
    segment_ids,
    ln1_gain,
    ln1_bias,
    w_qkv,
    b_qkv,
    w_out,
    ln2_gain,
    ln2_bias,
    w_gate_up,
    w_down,
    grad_out,
):
    dp = lax.axis_size("dp")
    chips = dp // 2
    block = D // dp
    width = w_qkv.shape[2]
    ff = w_gate_up.shape[2]
    heads = width // HEAD_DIM
    rank = lax.axis_index("tensor")
    me = lax.axis_index("dp")
    core = me % 2
    scale = HEAD_DIM ** (-0.5)
    bf = jnp.bfloat16

    order = ring_order(chips)
    place = {chip: i for i, chip in enumerate(order)}
    ring = []
    for i in range(chips):
        here, there = order[i], order[(i + 1) % chips]
        ring += [(2 * here, 2 * there), (2 * there + 1, 2 * here + 1)]
    siblings = [(i, i ^ 1) for i in range(dp)]
    targets = np.zeros((dp, chips), np.int32)
    for chip in range(chips):
        for s in range(chips):
            targets[2 * chip, s] = order[(place[chip] - 1 - s) % chips]
            targets[2 * chip + 1, s] = order[(place[chip] + 1 + s) % chips]
    my_targets = lax.dynamic_slice_in_dim(jnp.asarray(targets), me, 1, 0)[0]

    def swap_core(v):
        return lax.ppermute(v, "dp", siblings)

    def pair_rows(v):
        return jnp.concatenate([v, swap_core(v)], axis=0)

    def pair_blocks(v):
        cut = v.reshape(v.shape[0], chips, 2, block)
        even, odd = cut[:, :, 0], cut[:, :, 1]
        keep = jnp.where(core == 0, even, odd).transpose(1, 0, 2)
        give = jnp.where(core == 0, odd, even).transpose(1, 0, 2)
        return jnp.concatenate([keep, swap_core(give)], axis=1)

    def ring_sum(blocks, term):
        def local(s):
            return term(lax.dynamic_index_in_dim(blocks, my_targets[s], 0, keepdims=False))

        moving = local(0).astype(bf)
        for s in range(1, chips):
            moving = lax.ppermute(moving, "dp", ring).astype(jnp.float32) + local(s)
            if s < chips - 1:
                moving = moving.astype(bf)
        return moving

    def all_sum(v):
        v = v + swap_tensor(v)
        step = 1
        while step < dp:
            v = v + lax.ppermute(v, "dp", [(i, i ^ step) for i in range(dp)])
            step *= 2
        return v

    def gather_tokens(v):
        return jnp.concatenate([v, swap_tensor(v)], axis=0)

    def scatter_tokens(v):
        mine = v.shape[0] // 2
        return v[:mine] + swap_tensor(v[mine:].astype(bf)).astype(jnp.float32)

    first = jnp.concatenate(
        [w_qkv[0], w_qkv[1], w_qkv[2], w_out.T, w_gate_up[0]], axis=1
    )
    second = jnp.concatenate([w_gate_up[1], w_down.T], axis=1)
    first = lax.all_gather(first, "dp", axis=0, tiled=True)
    second = lax.all_gather(second, "dp", axis=0, tiled=True)
    qkv_full = first[:, : 3 * width]
    out_full = first[:, 3 * width : 4 * width]
    gate_full = first[:, 4 * width :]
    up_full = second[:, :ff]
    down_full = second[:, ff:]

    inputs = tokens.astype(jnp.float32)
    normed1, normal1, inverse1 = layer_forward(inputs, ln1_gain, ln1_bias)
    rows1 = gather_tokens(normed1.astype(bf))
    seq = rows1.shape[0]
    grad_rows = gather_tokens(grad_out)
    token_order = (jnp.arange(seq, dtype=jnp.int32) + rank * (seq // 2)) % seq
    own = segment_ids[0]
    half = seq // 2
    segments = jnp.where(
        rank == 0, own, jnp.concatenate([own[half:], own[:half]])
    )
    cosine, sine_table, visible = segment_tables(segments, token_order)
    bias_mine = lax.dynamic_slice_in_dim(
        b_qkv.astype(jnp.float32), rank * width, width, 1
    )

    projected = mm(rows1, qkv_full).reshape(seq, 3, width) + bias_mine[None]
    query_heads = projected[:, 0].reshape(seq, heads, HEAD_DIM)
    key_heads = projected[:, 1].reshape(seq, heads, HEAD_DIM)
    queries = rotate_heads(query_heads, cosine, sine_table, 1.0).astype(bf)
    key_rot = rotate_heads(key_heads, cosine, sine_table, 1.0).astype(bf)
    values = projected[:, 2].reshape(seq, heads, HEAD_DIM).astype(bf)
    raw_scores = (
        jnp.einsum("qhe,khe->hqk", queries, key_rot, preferred_element_type=jnp.float32) * scale
    )
    scores = jnp.where(visible[None], raw_scores, -1e30)
    row_top = jnp.max(scores, axis=-1, keepdims=True)
    exponent = jnp.exp(scores - row_top)
    row_total = jnp.sum(exponent, axis=-1, keepdims=True)
    attention = exponent / row_total
    attention_low = attention.astype(bf)
    context = jnp.einsum(
        "hqk,khe->qhe", attention_low, values, preferred_element_type=jnp.float32
    )
    context = context.astype(bf).reshape(seq, width)
    attended = scatter_tokens(mm(context, out_full, COLS))
    residual = inputs + attended
    normed2, normal2, inverse2 = layer_forward(residual, ln2_gain, ln2_bias)
    rows2 = gather_tokens(normed2.astype(bf))
    gate_part = mm(rows2, gate_full)
    up_part = mm(rows2, up_full)
    gate_sigmoid = jax.nn.sigmoid(gate_part)
    gate_swish = gate_part * gate_sigmoid
    hidden = (gate_swish * up_part).astype(bf)
    mlp_part = scatter_tokens(mm(hidden, down_full, COLS))
    output = (residual + mlp_part).astype(bf)

    hidden_pair = pair_rows(hidden)
    grad_blocks = pair_blocks(grad_rows)
    grad_down = ring_sum(grad_blocks, lambda a: mm(hidden_pair, a, ROWS))

    grad_hidden = mm(grad_rows, down_full)
    grad_gate = (
        grad_hidden * up_part * gate_sigmoid * (1.0 + gate_part * (1.0 - gate_sigmoid))
    ).astype(bf)
    grad_up = (grad_hidden * gate_swish).astype(bf)
    gate_pair = pair_rows(grad_gate)
    up_pair = pair_rows(grad_up)
    normed2_blocks = pair_blocks(rows2)
    grad_w_gate = ring_sum(normed2_blocks, lambda a: mm(a, gate_pair, ROWS))
    grad_w_up = ring_sum(normed2_blocks, lambda a: mm(a, up_pair, ROWS))

    grad_normed2 = scatter_tokens(mm(grad_gate, gate_full, COLS) + mm(grad_up, up_full, COLS))
    sums2 = all_sum(
        jnp.stack([jnp.sum(grad_normed2 * normal2, axis=0), jnp.sum(grad_normed2, axis=0)])
    )
    grad_residual = grad_out.astype(jnp.float32) + layer_backward(
        grad_normed2, normal2, inverse2, ln2_gain
    )
    resid_rows = gather_tokens(grad_residual.astype(bf))
    context_pair = pair_rows(context)
    resid_blocks = pair_blocks(resid_rows)
    grad_w_out = ring_sum(resid_blocks, lambda a: mm(context_pair, a, ROWS))
    grad_context = mm(resid_rows, out_full).astype(bf).reshape(seq, heads, HEAD_DIM)
    grad_values = jnp.einsum(
        "hqk,qhe->khe", attention_low, grad_context, preferred_element_type=jnp.float32
    )
    grad_attention = jnp.einsum(
        "qhe,khe->hqk", grad_context, values, preferred_element_type=jnp.float32
    )
    row_delta = jnp.sum(grad_attention * attention, axis=-1, keepdims=True)
    grad_scores = (attention * (grad_attention - row_delta)).astype(bf)
    grad_queries = (
        jnp.einsum("hqk,khe->qhe", grad_scores, key_rot, preferred_element_type=jnp.float32)
        * scale
    )
    grad_keys = (
        jnp.einsum("hqk,qhe->khe", grad_scores, queries, preferred_element_type=jnp.float32)
        * scale
    )
    grad_projected = jnp.concatenate(
        [
            rotate_heads(grad_queries, cosine, sine_table, -1.0).reshape(seq, width),
            rotate_heads(grad_keys, cosine, sine_table, -1.0).reshape(seq, width),
            grad_values.reshape(seq, width),
        ],
        axis=1,
    ).astype(bf)
    projected_pair = pair_rows(grad_projected)
    normed1_blocks = pair_blocks(rows1)
    grad_qkv = ring_sum(normed1_blocks, lambda a: mm(a, projected_pair, ROWS))
    bias_grad_mine = jnp.sum(grad_projected.astype(jnp.float32), axis=0).reshape(3, width)
    bias_grad_full = lax.dynamic_update_slice_in_dim(
        jnp.zeros(b_qkv.shape, jnp.float32), bias_grad_mine, rank * width, 1
    )
    grad_normed1 = scatter_tokens(mm(grad_projected, qkv_full, COLS))
    sums1 = all_sum(
        jnp.concatenate(
            [
                jnp.sum(grad_normed1 * normal1, axis=0)[None],
                jnp.sum(grad_normed1, axis=0)[None],
                bias_grad_full,
            ]
        )
    )
    grad_inputs = grad_residual + layer_backward(grad_normed1, normal1, inverse1, ln1_gain)
    return (
        output,
        grad_inputs.astype(bf),
        sums1[0],
        sums1[1],
        grad_qkv.reshape(block, 3, width).transpose(1, 0, 2),
        sums1[2:],
        grad_w_out,
        sums2[0],
        sums2[1],
        jnp.stack([grad_w_gate, grad_w_up]),
        grad_down,
    )


def solution(mesh):
    placed = (
        P(("dp", "tensor"), None),
        P("dp", None),
        P(),
        P(),
        P(None, "dp", "tensor"),
        P(),
        P("tensor", "dp"),
        P(),
        P(),
        P(None, "dp", "tensor"),
        P("tensor", "dp"),
        P(("dp", "tensor"), None),
    )
    return jax.shard_map(
        per_device,
        mesh=mesh,
        in_specs=placed,
        out_specs=(
            P(("dp", "tensor"), None),
            P(("dp", "tensor"), None),
            P(),
            P(),
            P(None, "dp", "tensor"),
            P(),
            P("tensor", "dp"),
            P(),
            P(),
            P(None, "dp", "tensor"),
            P("tensor", "dp"),
        ),
        check_vma=False,
    )
```

```python
import math

import jax
import jax.numpy as jnp
import numpy as np
from jax import lax
from jax.experimental import pallas as pl
from jax.experimental.pallas import tpu as pltpu
from jax.sharding import PartitionSpec as P


D = 2048
HEAD_DIM = 64
ROT_DIMS = 16
EPSILON = 1e-05
SWAP = [(0, 1), (1, 0)]
ROWS = (((0,), (0,)), ((), ()))
COLS = (((1,), (1,)), ((), ()))


def mm(a, b, dims=(((1,), (0,)), ((), ()))):
    return lax.dot_general(a, b, dims, preferred_element_type=jnp.float32)


def layer_forward(values, gain, shift):
    row_mean = jnp.mean(values, axis=-1, keepdims=True)
    centred = values - row_mean
    variance = jnp.mean(centred * centred, axis=-1, keepdims=True)
    inverse = lax.rsqrt(variance + EPSILON)
    normal = centred * inverse
    return (normal * gain.astype(jnp.float32) + shift.astype(jnp.float32), normal, inverse)


def layer_backward(grad_normed, normal, inverse, gain):
    scaled = grad_normed * gain.astype(jnp.float32)
    first_mean = jnp.mean(scaled, axis=-1, keepdims=True)
    second_mean = jnp.mean(scaled * normal, axis=-1, keepdims=True)
    return inverse * (scaled - first_mean - normal * second_mean)


def segment_tables(segments, order):
    earlier = jnp.sum((segments[None, :] < segments[:, None]).astype(jnp.int32), axis=1)
    position = order - earlier
    halfway = ROT_DIMS // 2
    frequency = jnp.exp(
        jnp.arange(halfway, dtype=jnp.float32) * (-2.0 * math.log(10000.0) / ROT_DIMS)
    )
    angles = position.astype(jnp.float32)[:, None] * frequency[None, :]
    visible = (order[None, :] <= order[:, None]) & (segments[None, :] == segments[:, None])
    return (jnp.cos(angles)[:, None, :], jnp.sin(angles)[:, None, :], visible)


def rotate_heads(values, cosine, sine_table, direction):
    halfway = ROT_DIMS // 2
    first_part = values[..., :halfway]
    second_part = values[..., halfway:ROT_DIMS]
    rest_part = values[..., ROT_DIMS:]
    return jnp.concatenate(
        [
            first_part * cosine - direction * second_part * sine_table,
            second_part * cosine + direction * first_part * sine_table,
            rest_part,
        ],
        axis=-1,
    )


def after(value, *earlier):
    return lax.optimization_barrier((value, *earlier))[0]


def ring_order(chips):
    half = chips // 2
    return [0] + [2 * i + 1 for i in range(half)] + [2 * i for i in range(half - 1, 0, -1)]


def order_kernel(columns, mine_ref, theirs_ref, out_ref):
    half = mine_ref.shape[0]
    out_ref[0, :half] = mine_ref[...]
    out_ref[0, half:] = theirs_ref[...]


def order_blocks(mine, theirs, columns, block):
    rows = mine.shape[0]
    count = columns.shape[0]
    if block % 128:
        both = jnp.concatenate([mine, theirs]).reshape(2 * rows, -1, block)
        return jnp.take(both, columns, axis=1).transpose(1, 0, 2)
    return pl.pallas_call(
        order_kernel,
        grid_spec=pltpu.PrefetchScalarGridSpec(
            num_scalar_prefetch=1,
            grid=(count,),
            in_specs=[pl.BlockSpec((rows, block), lambda i, c: (0, c[i]))] * 2,
            out_specs=pl.BlockSpec((1, 2 * rows, block), lambda i, c: (i, 0, 0)),
        ),
        out_shape=jax.ShapeDtypeStruct((count, 2 * rows, block), mine.dtype),
        cost_estimate=pl.CostEstimate(
            flops=0, bytes_accessed=8 * rows * count * block, transcendentals=0
        ),
        name="order_blocks",
    )(columns, mine, theirs)


def swap_tensor(v):
    return lax.ppermute(v, "tensor", SWAP)


def per_device(
    tokens,
    segment_ids,
    ln1_gain,
    ln1_bias,
    w_qkv,
    b_qkv,
    w_out,
    ln2_gain,
    ln2_bias,
    w_gate_up,
    w_down,
    grad_out,
):
    dp = lax.axis_size("dp")
    chips = dp // 2
    block = D // dp
    width = w_qkv.shape[2]
    ff = w_gate_up.shape[2]
    heads = width // HEAD_DIM
    rank = lax.axis_index("tensor")
    me = lax.axis_index("dp")
    core = me % 2
    scale = HEAD_DIM ** (-0.5)
    bf = jnp.bfloat16

    order = ring_order(chips)
    place = {chip: i for i, chip in enumerate(order)}
    ring = []
    for i in range(chips):
        here, there = order[i], order[(i + 1) % chips]
        ring += [(2 * here, 2 * there), (2 * there + 1, 2 * here + 1)]
    siblings = [(i, i ^ 1) for i in range(dp)]
    targets = np.zeros((dp, chips), np.int32)
    for chip in range(chips):
        for s in range(chips):
            targets[2 * chip, s] = order[(place[chip] - 1 - s) % chips]
            targets[2 * chip + 1, s] = order[(place[chip] + 1 + s) % chips]
    my_targets = lax.dynamic_slice_in_dim(jnp.asarray(targets), me, 1, 0)[0]

    def swap_core(v):
        return lax.ppermute(v, "dp", siblings)

    def pair_rows(v):
        return jnp.concatenate([v, swap_core(v)], axis=0)

    columns = 2 * my_targets + core

    def pair_blocks(v):
        return order_blocks(v, swap_core(v), columns, block)

    def ring_sum(blocks, term):
        moving = term(blocks[0]).astype(bf)
        for step in range(1, chips):
            moving = lax.ppermute(moving, "dp", ring)
            moving = moving.astype(jnp.float32) + term(blocks[step])
            if step < chips - 1:
                moving = moving.astype(bf)
        return moving

    def all_sum(v):
        v = v + swap_tensor(v)
        step = 1
        while step < dp:
            v = v + lax.ppermute(v, "dp", [(i, i ^ step) for i in range(dp)])
            step *= 2
        return v

    def gather_tokens(v):
        return jnp.concatenate([v, swap_tensor(v)], axis=0)

    def scatter_tokens(v):
        mine = v.shape[0] // 2
        return v[:mine] + swap_tensor(v[mine:].astype(bf)).astype(jnp.float32)

    part = ff // 2

    def gather_rows(pieces):
        packed = jnp.concatenate(pieces, axis=1)
        return lax.all_gather(packed, "dp", axis=0, tiled=True)

    first = gather_rows([w_qkv[0], w_qkv[1], w_qkv[2], w_out.T, w_gate_up[0, :, :128]])
    second = gather_rows([w_gate_up[0], w_gate_up[1, :, :part]])
    third = gather_rows([w_gate_up[1, :, part:], w_down.T])
    qkv_full = first[:, : 3 * width]
    out_full = first[:, 3 * width : 4 * width]
    gate_full = second[:, :ff]
    up_full = (second[:, ff:], third[:, : ff - part])
    down_full = (third[:, ff - part : ff], third[:, ff:])
    halves = (slice(0, part), slice(part, ff))

    inputs = tokens.astype(jnp.float32)
    normed1, normal1, inverse1 = layer_forward(inputs, ln1_gain, ln1_bias)
    rows1 = gather_tokens(normed1.astype(bf))
    seq = rows1.shape[0]
    grad_rows = gather_tokens(grad_out)
    token_order = (jnp.arange(seq, dtype=jnp.int32) + rank * (seq // 2)) % seq
    own = segment_ids[0]
    half = seq // 2
    segments = jnp.where(
        rank == 0, own, jnp.concatenate([own[half:], own[:half]])
    )
    cosine, sine_table, visible = segment_tables(segments, token_order)
    bias_mine = lax.dynamic_slice_in_dim(
        b_qkv.astype(jnp.float32), rank * width, width, 1
    )

    projected = mm(rows1, qkv_full).reshape(seq, 3, width) + bias_mine[None]
    query_heads = projected[:, 0].reshape(seq, heads, HEAD_DIM)
    key_heads = projected[:, 1].reshape(seq, heads, HEAD_DIM)
    queries = rotate_heads(query_heads, cosine, sine_table, 1.0).astype(bf)
    key_rot = rotate_heads(key_heads, cosine, sine_table, 1.0).astype(bf)
    values = projected[:, 2].reshape(seq, heads, HEAD_DIM).astype(bf)
    raw_scores = (
        jnp.einsum("qhe,khe->hqk", queries, key_rot, preferred_element_type=jnp.float32) * scale
    )
    scores = jnp.where(visible[None], raw_scores, -1e30)
    row_top = jnp.max(scores, axis=-1, keepdims=True)
    exponent = jnp.exp(scores - row_top)
    row_total = jnp.sum(exponent, axis=-1, keepdims=True)
    attention = exponent / row_total
    attention_low = attention.astype(bf)
    context = jnp.einsum(
        "hqk,khe->qhe", attention_low, values, preferred_element_type=jnp.float32
    )
    context = context.astype(bf).reshape(seq, width)
    attended = scatter_tokens(mm(context, out_full, COLS))
    residual = inputs + attended
    normed2, normal2, inverse2 = layer_forward(residual, ln2_gain, ln2_bias)
    rows2 = gather_tokens(normed2.astype(bf))
    grad_blocks = pair_blocks(grad_rows)
    normed2_blocks = pair_blocks(rows2)
    gate_part = mm(rows2, gate_full)
    hidden, hidden_pairs, gates, ups = [], [], [], []
    for i, cut in enumerate(halves):
        up = mm(after(rows2, *hidden), up_full[i])
        gate = gate_part[:, cut]
        gate, up, low = lax.optimization_barrier(
            (gate, up, (gate * jax.nn.sigmoid(gate) * up).astype(bf))
        )
        gates.append(gate)
        ups.append(up)
        hidden.append(low)
        hidden_pairs.append(pair_rows(hidden[i]))
    grad_downs = [
        ring_sum(grad_blocks, lambda a, h=hidden_pairs[i]: mm(h, a, ROWS))
        for i in range(2)
    ]
    grad_gates, grad_ups = [], []
    for i in range(2):
        grad_hidden = mm(after(grad_rows, *hidden, *grad_gates), down_full[i])
        gate, up = gates[i], ups[i]
        sigmoid = jax.nn.sigmoid(gate)
        grad_gates.append(
            (grad_hidden * up * sigmoid * (1.0 + gate * (1.0 - sigmoid))).astype(bf)
        )
        grad_ups.append((grad_hidden * (gate * sigmoid)).astype(bf))
    grad_gate = jnp.concatenate(grad_gates, axis=1)
    gate_pair = pair_rows(grad_gate)
    up_pair = pair_rows(jnp.concatenate(grad_ups, axis=1))
    grad_w_gate = ring_sum(normed2_blocks, lambda a: mm(a, gate_pair, ROWS))
    grad_w_up = ring_sum(normed2_blocks, lambda a: mm(a, up_pair, ROWS))
    grad_normed2 = mm(grad_gate, gate_full, COLS)
    for i in range(2):
        grad_normed2 += mm(grad_ups[i], up_full[i], COLS)
    grad_normed2 = scatter_tokens(grad_normed2)
    sums2 = all_sum(
        jnp.stack([jnp.sum(grad_normed2 * normal2, axis=0), jnp.sum(grad_normed2, axis=0)])
    )
    grad_residual = grad_out.astype(jnp.float32) + layer_backward(
        grad_normed2, normal2, inverse2, ln2_gain
    )
    resid_rows = gather_tokens(grad_residual.astype(bf))
    context_pair = pair_rows(context)
    resid_blocks = pair_blocks(resid_rows)
    grad_context = mm(resid_rows, out_full)
    grad_context = grad_context.astype(bf).reshape(seq, heads, HEAD_DIM)
    grad_values = jnp.einsum(
        "hqk,qhe->khe", attention_low, grad_context, preferred_element_type=jnp.float32
    )
    grad_attention = jnp.einsum(
        "qhe,khe->hqk", grad_context, values, preferred_element_type=jnp.float32
    )
    row_delta = jnp.sum(grad_attention * attention, axis=-1, keepdims=True)
    grad_scores = (attention * (grad_attention - row_delta)).astype(bf)
    grad_queries = (
        jnp.einsum("hqk,khe->qhe", grad_scores, key_rot, preferred_element_type=jnp.float32)
        * scale
    )
    grad_keys = (
        jnp.einsum("hqk,qhe->khe", grad_scores, queries, preferred_element_type=jnp.float32)
        * scale
    )
    grad_values = grad_values.reshape(seq, width).astype(bf)
    values_pair = pair_rows(grad_values)
    normed1_blocks = pair_blocks(rows1)

    grad_v = ring_sum(normed1_blocks, lambda a: mm(a, values_pair, ROWS))
    grad_w_out = ring_sum(resid_blocks, lambda a: mm(context_pair, a, ROWS))
    grad_qk = jnp.concatenate(
        [
            rotate_heads(grad_queries, cosine, sine_table, -1.0).reshape(seq, width),
            rotate_heads(grad_keys, cosine, sine_table, -1.0).reshape(seq, width),
        ],
        axis=1,
    ).astype(bf)
    qk_pair = pair_rows(grad_qk)
    grad_qk_sum = ring_sum(normed1_blocks, lambda a: mm(a, qk_pair, ROWS))
    grad_projected = jnp.concatenate([grad_qk, grad_values], axis=1)
    bias_grad_mine = jnp.sum(grad_projected.astype(jnp.float32), axis=0).reshape(3, width)
    bias_grad_full = lax.dynamic_update_slice_in_dim(
        jnp.zeros(b_qkv.shape, jnp.float32), bias_grad_mine, rank * width, 1
    )
    grad_normed1 = mm(grad_projected, qkv_full, COLS)
    grad_normed1 = scatter_tokens(grad_normed1)
    mlp_part = mm(hidden[0], down_full[0], COLS)
    mlp_part += mm(hidden[1], down_full[1], COLS)
    output = (residual + scatter_tokens(mlp_part)).astype(bf)
    sums1 = all_sum(
        jnp.concatenate(
            [
                jnp.sum(grad_normed1 * normal1, axis=0)[None],
                jnp.sum(grad_normed1, axis=0)[None],
                bias_grad_full,
            ]
        )
    )
    grad_inputs = grad_residual + layer_backward(grad_normed1, normal1, inverse1, ln1_gain)
    return (
        output,
        grad_inputs.astype(bf),
        sums1[0],
        sums1[1],
        jnp.stack([grad_qk_sum[:, :width], grad_qk_sum[:, width:], grad_v]),
        sums1[2:],
        grad_w_out,
        sums2[0],
        sums2[1],
        jnp.stack([grad_w_gate, grad_w_up]),
        jnp.concatenate(grad_downs),
    )


def solution(mesh):
    placed = (
        P(("dp", "tensor"), None),
        P("dp", None),
        P(),
        P(),
        P(None, "dp", "tensor"),
        P(),
        P("tensor", "dp"),
        P(),
        P(),
        P(None, "dp", "tensor"),
        P("tensor", "dp"),
        P(("dp", "tensor"), None),
    )
    return jax.shard_map(
        per_device,
        mesh=mesh,
        in_specs=placed,
        out_specs=(
            P(("dp", "tensor"), None),
            P(("dp", "tensor"), None),
            P(),
            P(),
            P(None, "dp", "tensor"),
            P(),
            P("tensor", "dp"),
            P(),
            P(),
            P(None, "dp", "tensor"),
            P("tensor", "dp"),
        ),
        check_vma=False,
    )
```

```python
import math

import jax
import jax.numpy as jnp
import numpy as np
from jax import lax
from jax.experimental import pallas as pl
from jax.experimental.pallas import tpu as pltpu
from jax.sharding import PartitionSpec as P


D = 2048
HEAD_DIM = 64
ROT_DIMS = 16
EPSILON = 1e-05
SWAP = [(0, 1), (1, 0)]
ROWS = (((0,), (0,)), ((), ()))
COLS = (((1,), (1,)), ((), ()))


def mm(a, b, dims=(((1,), (0,)), ((), ()))):
    return lax.dot_general(a, b, dims, preferred_element_type=jnp.float32)


def layer_forward(values, gain, shift):
    row_mean = jnp.mean(values, axis=-1, keepdims=True)
    centred = values - row_mean
    variance = jnp.mean(centred * centred, axis=-1, keepdims=True)
    inverse = lax.rsqrt(variance + EPSILON)
    normal = centred * inverse
    return (normal * gain.astype(jnp.float32) + shift.astype(jnp.float32), normal, inverse)


def layer_backward(grad_normed, normal, inverse, gain):
    scaled = grad_normed * gain.astype(jnp.float32)
    first_mean = jnp.mean(scaled, axis=-1, keepdims=True)
    second_mean = jnp.mean(scaled * normal, axis=-1, keepdims=True)
    return inverse * (scaled - first_mean - normal * second_mean)


def segment_tables(segments, order):
    earlier = jnp.sum((segments[None, :] < segments[:, None]).astype(jnp.int32), axis=1)
    position = order - earlier
    halfway = ROT_DIMS // 2
    frequency = jnp.exp(
        jnp.arange(halfway, dtype=jnp.float32) * (-2.0 * math.log(10000.0) / ROT_DIMS)
    )
    angles = position.astype(jnp.float32)[:, None] * frequency[None, :]
    visible = (order[None, :] <= order[:, None]) & (segments[None, :] == segments[:, None])
    return (jnp.cos(angles)[:, None, :], jnp.sin(angles)[:, None, :], visible)


def rotate_heads(values, cosine, sine_table, direction):
    halfway = ROT_DIMS // 2
    first_part = values[..., :halfway]
    second_part = values[..., halfway:ROT_DIMS]
    rest_part = values[..., ROT_DIMS:]
    return jnp.concatenate(
        [
            first_part * cosine - direction * second_part * sine_table,
            second_part * cosine + direction * first_part * sine_table,
            rest_part,
        ],
        axis=-1,
    )


def ring_order(chips):
    half = chips // 2
    return [0] + [2 * i + 1 for i in range(half)] + [2 * i for i in range(half - 1, 0, -1)]


def order_kernel(columns, mine_ref, theirs_ref, *out_refs):
    for i, out_ref in enumerate(out_refs):
        start = pl.multiple_of(columns[i] * 128, 128)
        out_ref[0] = mine_ref[:, pl.ds(start, 128)]
        out_ref[1] = theirs_ref[:, pl.ds(start, 128)]


def order_blocks(mine, theirs, columns, block):
    rows, width = mine.shape
    count = columns.shape[0]
    if block != 128:
        both = jnp.concatenate([mine, theirs]).reshape(2 * rows, -1, block)
        return [jnp.take(both, columns[i], axis=1) for i in range(count)]
    tile = rows // 2
    blocks = pl.pallas_call(
        order_kernel,
        grid_spec=pltpu.PrefetchScalarGridSpec(
            num_scalar_prefetch=1,
            grid=(2,),
            in_specs=[pl.BlockSpec((tile, width), lambda i, c: (i, 0))] * 2,
            out_specs=[pl.BlockSpec((2, tile, block), lambda i, c: (0, i, 0))] * count,
        ),
        out_shape=[jax.ShapeDtypeStruct((2, rows, block), mine.dtype)] * count,
        cost_estimate=pl.CostEstimate(
            flops=0, bytes_accessed=8 * rows * count * block, transcendentals=0
        ),
        name="order_blocks",
    )(columns, mine, theirs)
    return [item.reshape(2 * rows, block) for item in blocks]


def after(value, *earlier):
    return lax.optimization_barrier((value, *earlier))[0]


class Ring:
    def __init__(self, pairs, blocks, term, earlier=()):
        self.pairs, self.blocks, self.term, self.steps = pairs, blocks, term, 1
        self.sent = term(after(blocks[0], *earlier)).astype(jnp.bfloat16)

    def step(self, *earlier):
        if self.steps < len(self.blocks):
            came = lax.ppermute(self.sent, "dp", self.pairs).astype(jnp.float32)
            self.sent = came + self.term(after(self.blocks[self.steps], *earlier))
            self.steps += 1
            if self.steps < len(self.blocks):
                self.sent = self.sent.astype(jnp.bfloat16)
        return self.sent


def swap_tensor(v):
    return lax.ppermute(v, "tensor", SWAP)


def per_device(
    tokens,
    segment_ids,
    ln1_gain,
    ln1_bias,
    w_qkv,
    b_qkv,
    w_out,
    ln2_gain,
    ln2_bias,
    w_gate_up,
    w_down,
    grad_out,
):
    dp = lax.axis_size("dp")
    chips = dp // 2
    block = D // dp
    width = w_qkv.shape[2]
    ff = w_gate_up.shape[2]
    heads = width // HEAD_DIM
    rank = lax.axis_index("tensor")
    me = lax.axis_index("dp")
    scale = HEAD_DIM ** (-0.5)
    bf = jnp.bfloat16

    order = ring_order(chips)
    place = {chip: i for i, chip in enumerate(order)}
    ring = []
    for i in range(chips):
        here, there = order[i], order[(i + 1) % chips]
        ring += [(2 * here, 2 * there), (2 * there + 1, 2 * here + 1)]
    siblings = [(i, i ^ 1) for i in range(dp)]
    targets = np.zeros((dp, chips), np.int32)
    for chip in range(chips):
        for s in range(chips):
            targets[2 * chip, s] = order[(place[chip] - 1 - s) % chips]
            targets[2 * chip + 1, s] = order[(place[chip] + 1 + s) % chips]
    columns_of = jnp.asarray(2 * targets + np.arange(dp, dtype=np.int32)[:, None] % 2)
    columns = columns_of[me]

    def swap_core(v):
        return lax.ppermute(v, "dp", siblings)

    def pair_rows(v):
        return jnp.concatenate([v, swap_core(v)], axis=0)

    def pair_blocks(v):
        return order_blocks(v, swap_core(v), columns, block)

    def all_sum(*rows):
        packed = jnp.concatenate([row.reshape(-1) for row in rows]).reshape(-1, 128)
        gathered = lax.all_gather(packed, ("dp", "tensor"), axis=0, tiled=True)
        return jnp.sum(gathered.reshape(dp, -1, packed.size), axis=0)

    def gather_tokens(v):
        return jnp.concatenate([v, swap_tensor(v)], axis=0)

    def scatter_tokens(v, meanwhile=None):
        mine = v.shape[0] // 2
        give = v[mine:].astype(bf)
        extra = meanwhile and meanwhile(give)
        total = v[:mine] + swap_tensor(give).astype(jnp.float32)
        return (total, extra) if meanwhile else total

    part = ff // 2

    def gather_rows(pieces):
        packed = jnp.concatenate(pieces, axis=1)
        return lax.all_gather(packed, "dp", axis=0, tiled=True)

    first = gather_rows([w_qkv[0], w_qkv[1], w_qkv[2], w_out.T, w_gate_up[0, :, :128]])
    halves = [
        gather_rows(
            [
                w_gate_up[0, :, i * part : (i + 1) * part],
                w_gate_up[1, :, i * part : (i + 1) * part],
                w_down[i * part : (i + 1) * part].T,
            ],
        )
        for i in range(2)
    ]
    qkv_full = first[:, : 3 * width]
    out_full = first[:, 3 * width : 4 * width]
    gate_up_full = [half[:, : 2 * part] for half in halves]
    down_full = [half[:, 2 * part :] for half in halves]

    inputs = tokens.astype(jnp.float32)
    normed1, normal1, inverse1 = layer_forward(inputs, ln1_gain, ln1_bias)
    rows1 = gather_tokens(normed1.astype(bf))
    seq = rows1.shape[0]
    grad_rows = gather_tokens(grad_out)
    token_order = (jnp.arange(seq, dtype=jnp.int32) + rank * (seq // 2)) % seq
    own = segment_ids[0]
    half = seq // 2
    segments = jnp.where(
        rank == 0, own, jnp.concatenate([own[half:], own[:half]])
    )
    cosine, sine_table, visible = segment_tables(segments, token_order)
    bias_mine = lax.dynamic_slice_in_dim(
        b_qkv.astype(jnp.float32), rank * width, width, 1
    )

    projected = mm(rows1, qkv_full).reshape(seq, 3, width) + bias_mine[None]
    query_heads = projected[:, 0].reshape(seq, heads, HEAD_DIM)
    key_heads = projected[:, 1].reshape(seq, heads, HEAD_DIM)
    queries = rotate_heads(query_heads, cosine, sine_table, 1.0).astype(bf)
    key_rot = rotate_heads(key_heads, cosine, sine_table, 1.0).astype(bf)
    values = projected[:, 2].reshape(seq, heads, HEAD_DIM).astype(bf)
    raw_scores = (
        jnp.einsum("qhe,khe->hqk", queries, key_rot, preferred_element_type=jnp.float32) * scale
    )
    scores = jnp.where(visible[None], raw_scores, -1e30)
    row_top = jnp.max(scores, axis=-1, keepdims=True)
    exponent = jnp.exp(scores - row_top)
    row_total = jnp.sum(exponent, axis=-1, keepdims=True)
    attention = exponent / row_total
    attention_low = attention.astype(bf)
    context = jnp.einsum(
        "hqk,khe->qhe", attention_low, values, preferred_element_type=jnp.float32
    )
    context = context.astype(bf).reshape(seq, width)
    attended = scatter_tokens(mm(context, out_full, COLS))
    residual = inputs + attended
    normed2, normal2, inverse2 = layer_forward(residual, ln2_gain, ln2_bias)
    rows2 = gather_tokens(normed2.astype(bf))
    grad_blocks = pair_blocks(grad_rows)
    normed2_blocks = pair_blocks(rows2)
    normed1_blocks = pair_blocks(rows1)
    context_pair = pair_rows(context)

    def forward_half(i, rows):
        gate_up = mm(rows, gate_up_full[i])
        gate, up = gate_up[:, :part], gate_up[:, part:]
        low = (gate * jax.nn.sigmoid(gate) * up).astype(bf)
        return lax.optimization_barrier((gate_up, low))

    def backward_half(i, rows, gate_up):
        grad_hidden = mm(rows, down_full[i])
        gate, up = gate_up[:, :part], gate_up[:, part:]
        sigmoid = jax.nn.sigmoid(gate)
        grad_gate = grad_hidden * up * sigmoid * (1.0 + gate * (1.0 - sigmoid))
        return lax.optimization_barrier(
            jnp.concatenate([grad_gate, grad_hidden * (gate * sigmoid)], axis=1).astype(bf)
        )

    rows2 = after(rows2, *grad_blocks, *normed2_blocks, *normed1_blocks, context_pair)
    gate_up0, hidden0 = forward_half(0, rows2)
    hidden_pair0 = pair_rows(hidden0)
    down0 = Ring(ring, grad_blocks, lambda a: mm(hidden_pair0, a, ROWS))
    grads0 = backward_half(0, after(grad_rows, down0.sent), gate_up0)
    grads_pair0 = pair_rows(grads0)
    mark = down0.step(grads0)
    both0 = Ring(ring, normed2_blocks, lambda a: mm(a, grads_pair0, ROWS), (mark,))
    grad_normed2 = mm(after(grads0, both0.sent), gate_up_full[0], COLS)
    mark = down0.step(grad_normed2)
    mlp_part = mm(after(hidden0, mark), down_full[0], COLS)
    mark = both0.step(mlp_part)
    mark = down0.step(mark)
    mark = down0.step(mark)
    mark = both0.step(mark)
    mark = down0.step(mark)

    gate_up1, hidden1 = forward_half(1, after(rows2, mark))
    hidden_pair1 = pair_rows(hidden1)
    mark = down0.step(hidden1)
    mark = both0.step(mark)
    grads1 = backward_half(1, after(grad_rows, mark), gate_up1)
    grads_pair1 = pair_rows(grads1)
    down1 = Ring(ring, grad_blocks, lambda a: mm(hidden_pair1, a, ROWS), (grads1,))
    grad_normed2 += mm(after(grads1, down1.sent), gate_up_full[1], COLS)

    def first_wait(given):
        both = Ring(ring, normed2_blocks, lambda a: mm(a, grads_pair1, ROWS), (given,))
        down1.step(both.sent)
        return both

    grad_normed2, both1 = scatter_tokens(grad_normed2, first_wait)
    grad_residual = grad_out.astype(jnp.float32) + layer_backward(
        grad_normed2, normal2, inverse2, ln2_gain
    )
    resid_low = grad_residual.astype(bf)
    resid_rows = gather_tokens(resid_low)
    mark = both0.step(resid_low)
    mark = down1.step(mark)
    grad_context = mm(after(resid_rows, mark), out_full)
    grad_context = grad_context.astype(bf).reshape(seq, heads, HEAD_DIM)
    grad_values = jnp.einsum(
        "hqk,qhe->khe", attention_low, grad_context, preferred_element_type=jnp.float32
    )
    grad_attention = jnp.einsum(
        "qhe,khe->hqk", grad_context, values, preferred_element_type=jnp.float32
    )
    row_delta = jnp.sum(grad_attention * attention, axis=-1, keepdims=True)
    grad_scores = (attention * (grad_attention - row_delta)).astype(bf)
    mark = both1.step(grad_scores)
    mark = down1.step(mark)
    grad_scores = after(grad_scores, mark)
    grad_queries = (
        jnp.einsum("hqk,khe->qhe", grad_scores, key_rot, preferred_element_type=jnp.float32)
        * scale
    )
    grad_keys = (
        jnp.einsum("hqk,qhe->khe", grad_scores, queries, preferred_element_type=jnp.float32)
        * scale
    )
    grad_projected = jnp.concatenate(
        [
            rotate_heads(grad_queries, cosine, sine_table, -1.0).reshape(seq, width),
            rotate_heads(grad_keys, cosine, sine_table, -1.0).reshape(seq, width),
            grad_values.reshape(seq, width),
        ],
        axis=1,
    ).astype(bf)
    last_pair = pair_rows(grad_projected)
    mark = both0.step(grad_projected)
    last = Ring(ring, normed1_blocks, lambda a: mm(a, last_pair, ROWS), (mark,))
    resid_blocks = pair_blocks(after(resid_rows, last.sent))
    outs = Ring(ring, resid_blocks, lambda a: mm(context_pair, a, ROWS))
    mark = both1.step(outs.sent)
    mark = down1.step(mark)
    grad_normed1 = mm(after(grad_projected, mark), qkv_full, COLS)
    mark = both0.step(grad_normed1)
    mark = last.step(mark)
    mark = both1.step(mark)
    mark = outs.step(mark)
    mark = down1.step(mark)
    mlp_part += mm(after(hidden1, mark), down_full[1], COLS)
    grad_normed1 = scatter_tokens(grad_normed1)
    output = (residual + scatter_tokens(mlp_part)).astype(bf)
    grad_inputs = grad_residual + layer_backward(grad_normed1, normal1, inverse1, ln1_gain)
    for _ in range(chips):
        for stream in (last, both1, outs, both0, down1, down0):
            mark = stream.step(mark)
    last_sum = last.sent
    grad_gate_up = [
        jnp.concatenate([both0.sent[:, cut], both1.sent[:, cut]], axis=1)
        for cut in (slice(0, part), slice(part, 2 * part))
    ]
    sums = all_sum(
        jnp.sum(grad_normed1 * normal1, axis=0),
        jnp.sum(grad_normed1, axis=0),
        jnp.sum(grad_normed2 * normal2, axis=0),
        jnp.sum(grad_normed2, axis=0),
        jnp.sum(grad_projected.astype(jnp.float32), axis=0),
    )
    norms = jnp.sum(sums[:, : 4 * D], axis=0).reshape(4, D)
    biases = sums[:, 4 * D :].reshape(-1, 3, width).transpose(1, 0, 2).reshape(3, -1)
    return (
        output,
        grad_inputs.astype(bf),
        norms[0],
        norms[1],
        last_sum.reshape(block, 3, width).transpose(1, 0, 2),
        biases,
        outs.sent,
        norms[2],
        norms[3],
        jnp.stack(grad_gate_up),
        jnp.concatenate([down0.sent, down1.sent]),
    )


def solution(mesh):
    placed = (
        P(("dp", "tensor"), None),
        P("dp", None),
        P(),
        P(),
        P(None, "dp", "tensor"),
        P(),
        P("tensor", "dp"),
        P(),
        P(),
        P(None, "dp", "tensor"),
        P("tensor", "dp"),
        P(("dp", "tensor"), None),
    )
    return jax.shard_map(
        per_device,
        mesh=mesh,
        in_specs=placed,
        out_specs=(
            P(("dp", "tensor"), None),
            P(("dp", "tensor"), None),
            P(),
            P(),
            P(None, "dp", "tensor"),
            P(),
            P("tensor", "dp"),
            P(),
            P(),
            P(None, "dp", "tensor"),
            P("tensor", "dp"),
        ),
        check_vma=False,
    )
```
